32 devices in a mesh: dp: 2 (over core), seq: 16 (over z, y, x).
Axes of the slice: x: 2, y: 2, z: 4, core: 2. Of those that a mesh axis runs over, the one named last changes fastest.
Arguments:
- siblings: int32 [2, 32, 16], P('dp', 'seq'), may hold values from 0 to 31, all different within a row
- queries: bfloat16 [2, 32, 512, 2560], P('dp', 'seq'), may hold values from -6 to 6
- grad_out: bfloat16 [2, 32, 512, 2560], P('dp', 'seq'), may hold values from -6 to 6
- keys_in: bfloat16 [2, 32, 16, 512], P('dp', 'seq'), may hold values from -4 to 4
- input_values: bfloat16 [2, 32, 16, 512], P('dp', 'seq'), may hold values from -6 to 6
- summary: bfloat16 [2, 32, 16, 5120], P('dp', 'seq'), may hold values from -6 to 6
Outputs:
- query_gradient: bfloat16 [2, 32, 512, 2560], P('dp', 'seq')
- kv_weight_grad: float32 [5120, 1024], P(('dp', 'seq'))
The draws below stay inside these ranges and needn't reach their ends.
Inputs may be any that keep to these rules, and one draw needn't show every extreme that they name: `siblings`: the 16 entries of one completion's list are distinct completions of the same prompt.
All inputs are finite; a program needn't handle non-finite values.
Results may differ from the reference program's by a relative error of at most 0.012.
Values may be sent and summed in bfloat16 or wider, within the bound.
No kernel may reach another device: no remote copies, remote signals or barrier semaphores. Data moves between devices by JAX's collectives and lax.ppermute only.
A program may use at most 192 MiB of HBM per device.

```python
import math
import jax
import jax.numpy as jnp
from jax import lax

D = 5120
QUERY_HEADS = 20
KEY_VALUE_HEADS = 4
HEAD_SIZE = 128
SIB = 16
TQ = 512
SHARED_ROWS = 16
COMPLETION_COUNT = 32
PROMPT_COUNT = 2


def draw_queries(key, part):
    draw_key = jax.random.fold_in(key, 11)
    span_length = (PROMPT_COUNT, COMPLETION_COUNT, TQ, QUERY_HEADS * HEAD_SIZE)
    drawn = jnp.clip(jax.random.normal(draw_key, span_length, jnp.float32), -6.0, 6.0)
    return drawn.astype(jnp.bfloat16)


def draw_keys_in(key, part):
    draw_key = jax.random.fold_in(key, 13)
    span_length = (PROMPT_COUNT, COMPLETION_COUNT, SHARED_ROWS, KEY_VALUE_HEADS * HEAD_SIZE)
    drawn = jnp.clip(jax.random.normal(draw_key, span_length, jnp.float32), -4.0, 4.0)
    return drawn.astype(jnp.bfloat16)


def shard_levels(own_key, shape, pieces, smallest, top_value):
    gain = 1.0
    for axis_at, shards_of in pieces:
        steps = jax.random.uniform(jax.random.fold_in(jax.random.fold_in(own_key, 6), axis_at), (shards_of,), jnp.float32, smallest / len(pieces), top_value / len(pieces))
        gain = gain * jnp.repeat(jnp.exp(steps), shape[axis_at] // shards_of).reshape((-1,) + (1,) * (len(shape) - 1 - axis_at))
    return gain


def distinct(stream_key, rows, number_of, top, lift):
    ranking = jax.random.permutation(jax.random.fold_in(stream_key, 1), number_of)
    favour = ranking
    for power in range(3):
        favour = favour * favour // number_of
    favour = favour * lift // number_of
    tickets = jax.random.randint(jax.random.fold_in(stream_key, 2), (rows, number_of), 0, 4096) + favour
    fixed_rows = jax.random.permutation(jax.random.fold_in(stream_key, 3), rows)[jnp.arange(number_of) % rows]
    tickets = jnp.where(jnp.arange(rows)[:, None] == fixed_rows[None, :], 1 << 14, tickets)
    merit = tickets * number_of + jnp.arange(number_of)
    return lax.top_k(merit.astype(jnp.int32), top)[1].astype(jnp.int32)


def scatter_about(stream_key, dims, width, limit, pieces=(), kind=jnp.bfloat16):
    gain = shard_levels(stream_key, dims, pieces, -0.22, 0.18) if pieces else 1.0
    values = jax.random.normal(stream_key, dims, jnp.float32) * width * gain
    return jnp.minimum(jnp.maximum(values, -limit), limit).astype(kind)


def setup_inputs(seed: int = 0) -> dict:
    key_list = jax.random.split(jax.random.key(seed), 7)
    return {
        "siblings": distinct(key_list[0], PROMPT_COUNT * COMPLETION_COUNT, COMPLETION_COUNT, SIB, 8192).reshape((PROMPT_COUNT, COMPLETION_COUNT, SIB)),
        "queries": draw_queries(jax.random.fold_in(key_list[6], 71), 0),
        "grad_out": scatter_about(key_list[2], (PROMPT_COUNT, COMPLETION_COUNT, TQ, QUERY_HEADS * HEAD_SIZE), 1.0, 6.0, ((0, 2), (1, 16))),
        "keys_in": draw_keys_in(jax.random.fold_in(key_list[6], 71), 0),
        "input_values": scatter_about(key_list[4], (PROMPT_COUNT, COMPLETION_COUNT, SHARED_ROWS, KEY_VALUE_HEADS * HEAD_SIZE), 1.0, 6.0, ((0, 2), (1, 16))),
        "summary": scatter_about(key_list[5], (PROMPT_COUNT, COMPLETION_COUNT, SHARED_ROWS, D), 1.0, 6.0, ((0, 2), (1, 16))),
    }


def attend(query_tile_block, incoming_gradient, key_tile_block, value_tile_block):
    row_length = query_tile_block.shape[0]
    scaling = 1.0 / math.sqrt(HEAD_SIZE)
    query_float = query_tile_block.reshape(row_length, KEY_VALUE_HEADS, QUERY_HEADS // KEY_VALUE_HEADS, HEAD_SIZE).astype(jnp.float32)
    incoming_float = incoming_gradient.reshape(row_length, KEY_VALUE_HEADS, QUERY_HEADS // KEY_VALUE_HEADS, HEAD_SIZE).astype(jnp.float32)
    keys_float = key_tile_block.reshape(-1, KEY_VALUE_HEADS, HEAD_SIZE).astype(jnp.float32)
    values_float = value_tile_block.reshape(-1, KEY_VALUE_HEADS, HEAD_SIZE).astype(jnp.float32)
    scores = jnp.einsum('tgrd,lgd->grtl', query_float, keys_float) * scaling
    largest = lax.optimization_barrier(jnp.max(scores, axis=-1, keepdims=True))
    exponent = jnp.exp(scores - largest)
    probability = exponent / lax.optimization_barrier(jnp.sum(exponent, axis=-1, keepdims=True))
    prob_half = lax.optimization_barrier(probability.astype(jnp.bfloat16)).astype(jnp.float32)
    attended = jnp.einsum('grtl,lgd->grtd', prob_half, values_float)
    upstream_t = jnp.transpose(incoming_float, (1, 2, 0, 3))
    row_delta = lax.optimization_barrier(jnp.sum(upstream_t * attended, axis=-1, keepdims=True))
    prob_grad = jnp.einsum('grtd,lgd->grtl', upstream_t, values_float)
    score_grad = probability * (prob_grad - row_delta)
    score_half = lax.optimization_barrier(score_grad.astype(jnp.bfloat16)).astype(jnp.float32)
    query_gradient = jnp.einsum('grtl,lgd->tgrd', score_half, keys_float) * scaling
    key_gradient = jnp.einsum('grtl,tgrd->lgd', score_half, query_float) * scaling
    value_gradient = jnp.einsum('grtl,grtd->lgd', prob_half, upstream_t)
    return (query_gradient.reshape(row_length, QUERY_HEADS * HEAD_SIZE).astype(jnp.bfloat16), key_gradient.reshape(-1, KEY_VALUE_HEADS * HEAD_SIZE), value_gradient.reshape(-1, KEY_VALUE_HEADS * HEAD_SIZE))

def reference(siblings, queries, grad_out, keys_in, input_values, summary):
    key_value_width = KEY_VALUE_HEADS * HEAD_SIZE
    query_grads = []
    weight_total = jnp.zeros((D, 2 * key_value_width), jnp.float32)
    for prompt in range(PROMPT_COUNT):
        sibling = siblings[prompt]

        def per_member(member):
            chosen = sibling[member]
            key_tile_block = keys_in[prompt][chosen].reshape(SIB * SHARED_ROWS, key_value_width)
            value_tile_block = input_values[prompt][chosen].reshape(SIB * SHARED_ROWS, key_value_width)
            return attend(queries[prompt, member], grad_out[prompt, member], key_tile_block, value_tile_block)
        query_gradient, key_parts, value_parts = lax.map(per_member, jnp.arange(COMPLETION_COUNT, dtype=jnp.int32))
        owners = sibling.reshape(-1).astype(jnp.int32)
        key_total = jnp.zeros((COMPLETION_COUNT, SHARED_ROWS, key_value_width), jnp.float32).at[owners].add(key_parts.reshape(COMPLETION_COUNT * SIB, SHARED_ROWS, key_value_width))
        value_total = jnp.zeros((COMPLETION_COUNT, SHARED_ROWS, key_value_width), jnp.float32).at[owners].add(value_parts.reshape(COMPLETION_COUNT * SIB, SHARED_ROWS, key_value_width))
        grads_half = jnp.concatenate([key_total.astype(jnp.bfloat16), value_total.astype(jnp.bfloat16)], axis=-1).reshape(COMPLETION_COUNT * SHARED_ROWS, 2 * key_value_width)
        hidden = summary[prompt].reshape(COMPLETION_COUNT * SHARED_ROWS, D)
        weight_total = weight_total + jnp.dot(hidden.T, grads_half, preferred_element_type=jnp.float32)
        query_grads.append(query_gradient)
    return (jnp.stack(query_grads), weight_total)
```

```python
import math

import jax
import jax.numpy as jnp
from jax import lax
from jax.experimental import pallas as pl
from jax.experimental.pallas import tpu as pltpu
from jax.sharding import PartitionSpec as P

HEAD = 128
OUTER = 4
F32 = jnp.float32
BF16 = jnp.bfloat16


def dg(a, b, ca, cb):
    return lax.dot_general(a, b, (((ca,), (cb,)), ((), ())), preferred_element_type=F32)


def attention(idx, queries, grad_out, kv_parts):
    own, length, width = queries.shape
    inner = len(kv_parts)
    blocks, pos, kvw2 = kv_parts[0].shape
    kv_heads = kvw2 // (2 * HEAD)
    group = width // (kv_heads * HEAD)
    sib = idx.shape[1]
    rows = sib * pos
    scale = 1.0 / math.sqrt(HEAD)
    scale2 = scale * math.log2(math.e)

    def kern(idx_ref, q_ref, g_ref, *refs):
        kv_in = refs[:inner]
        dq_ref = refs[inner]
        outs = refs[inner + 1 : 2 * inner + 1]
        kv_s, k_s, v_s, acc = refs[2 * inner + 1 :]
        g = pl.program_id(0)
        c = pl.program_id(1)

        @pl.when((g == 0) & (c == 0))
        def _():
            for i in range(inner):
                kv_s[i * blocks : (i + 1) * blocks] = kv_in[i][...]

        k_at = pl.ds(pl.multiple_of(g * HEAD, HEAD), HEAD)
        v_at = pl.ds(pl.multiple_of((kv_heads + g) * HEAD, HEAD), HEAD)
        for j in range(sib):
            b = idx_ref[c, j]
            k_s[j * pos : (j + 1) * pos, :] = kv_s[b, :, k_at]
            v_s[j * pos : (j + 1) * pos, :] = kv_s[b, :, v_at]
        k = k_s[...]
        v = v_s[...]
        dk = dv = None
        for h in range(group):
            at = slice(h * HEAD, (h + 1) * HEAD)
            q = q_ref[0, :, at]
            go = g_ref[0, :, at]
            s = dg(k, q, 1, 1)
            m = jnp.max(s, axis=0, keepdims=True)
            e = jnp.exp2((s - m) * scale2)
            p = e * (1.0 / jnp.sum(e, axis=0, keepdims=True))
            ph = p.astype(BF16)
            dp = dg(v, go, 1, 1)
            delta = jnp.sum(ph.astype(F32) * dp, axis=0, keepdims=True)
            sh = (p * (dp - delta)).astype(BF16)
            dq_ref[0, :, at] = (dg(sh, k, 0, 0) * scale).astype(BF16)
            dkh = dg(sh, q, 1, 0)
            dvh = dg(ph, go, 1, 0)
            dk = dkh if dk is None else dk + dkh
            dv = dvh if dv is None else dv + dvh

        @pl.when(c == 0)
        def _():
            acc[...] = jnp.zeros_like(acc)

        for j in range(sib):
            b = idx_ref[c, j]
            acc[b, :, :HEAD] += dk[j * pos : (j + 1) * pos, :] * scale
            acc[b, :, HEAD:] += dv[j * pos : (j + 1) * pos, :]

        @pl.when(c == own - 1)
        def _():
            for i in range(inner):
                outs[i][...] = acc[i * blocks : (i + 1) * blocks].astype(BF16)

    q_spec = pl.BlockSpec((1, length, group * HEAD), lambda g, c, i: (c, 0, g))
    kv_spec = pl.BlockSpec(
        (blocks, pos, kvw2), lambda g, c, i: (0, 0, 0), pipeline_mode=pl.Buffered(1)
    )
    out_spec = pl.BlockSpec((blocks, pos, 2 * HEAD), lambda g, c, i: (0, 0, g))
    flops = 10 * own * length * group * kv_heads * rows * HEAD
    res = pl.pallas_call(
        kern,
        grid_spec=pltpu.PrefetchScalarGridSpec(
            num_scalar_prefetch=1,
            grid=(kv_heads, own),
            in_specs=[q_spec, q_spec] + [kv_spec] * inner,
            out_specs=[q_spec] + [out_spec] * inner,
            scratch_shapes=[
                pltpu.VMEM((inner * blocks, pos, kvw2), BF16),
                pltpu.VMEM((rows, HEAD), BF16),
                pltpu.VMEM((rows, HEAD), BF16),
                pltpu.VMEM((inner * blocks, pos, 2 * HEAD), F32),
            ],
        ),
        out_shape=[jax.ShapeDtypeStruct(queries.shape, BF16)]
        + [jax.ShapeDtypeStruct((blocks, pos, kvw2), BF16)] * inner,
        compiler_params=pltpu.CompilerParams(vmem_limit_bytes=48 << 20),
        cost_estimate=pl.CostEstimate(
            flops=flops, bytes_accessed=6 * queries.size, transcendentals=0
        ),
        name="attention",
    )(idx, queries, grad_out, *kv_parts)
    return res[0], res[1:]


def add_split(parts, pieces):
    shape = parts[0].shape
    each = shape[0] // pieces
    count = len(parts)

    def kern(*refs):
        for i in range(pieces):
            at = slice(i * each, (i + 1) * each)
            total = refs[0][at].astype(F32)
            for r in refs[1:count]:
                total = total + r[at].astype(F32)
            refs[count + i][...] = total.astype(BF16)

    return pl.pallas_call(
        kern,
        out_shape=[jax.ShapeDtypeStruct((each,) + shape[1:], BF16)] * pieces,
        cost_estimate=pl.CostEstimate(flops=0, bytes_accessed=2 * count * 2 * 65536, transcendentals=0),
        name="add_split",
    )(*parts)


def weight_parts(place, columns, grads, kv_heads):
    devices, dps, rows, width = columns.shape
    inner = len(grads)
    kvw2 = grads[0].shape[1]

    def kern(place_ref, c_ref, *refs):
        g_in = refs[:inner]
        outs = refs[inner : inner + dps]
        g_s, c_s = refs[inner + dps :]
        mine = place_ref[0]
        at = 0
        for i in range(inner):
            g_s[i * OUTER * rows : (i + 1) * OUTER * rows, :] = g_in[i][...]
        for k in range(dps):
            which = place_ref[1 + k]
            for i in range(inner):
                for o in range(OUTER):
                    at = (i * OUTER + o) * rows
                    c_s[at : at + rows, :] = c_ref[place_ref[1 + dps + i * OUTER + o], which]
            both = dg(c_s[...], g_s[...], 0, 0)
            for h in range(kv_heads):
                lo = 2 * h * HEAD
                outs[k][:, h * HEAD : (h + 1) * HEAD] = both[:, lo : lo + HEAD]
                outs[k][:, (kv_heads + h) * HEAD : (kv_heads + h + 1) * HEAD] = both[
                    :, lo + HEAD : lo + 2 * HEAD
                ]

    vmem = pl.BlockSpec(memory_space=pltpu.VMEM)
    return pl.pallas_call(
        kern,
        in_specs=[pl.BlockSpec(memory_space=pltpu.SMEM)] + [vmem] * (1 + inner),
        out_specs=[vmem] * dps,
        out_shape=[jax.ShapeDtypeStruct((width, kvw2), F32)] * dps,
        scratch_shapes=[
            pltpu.VMEM((devices * rows, kvw2), BF16),
            pltpu.VMEM((devices * rows, width), BF16),
        ],
        compiler_params=pltpu.CompilerParams(vmem_limit_bytes=32 << 20),
        name="weight_parts",
    )(place, columns, *grads)


def make_per_device(n_seq, n_dp):
    inner = n_seq // OUTER

    def swap(x, axis, count, by):
        return lax.ppermute(x, axis, [(i, i ^ by) for i in range(count)])

    def seq_swap(x, by):
        return swap(x, "seq", n_seq, by)

    def gather_all(x):
        near = [x] + [seq_swap(x, k * inner) for k in range(1, OUTER)]
        near = jnp.concatenate(near, axis=0)
        return [near] + [seq_swap(near, k) for k in range(1, inner)]

    def per_device(siblings, queries, grad_out, keys_in, input_values, summary):
        own, pos, kvw = keys_in.shape[1:]
        kv_heads = kvw // HEAD
        me = lax.axis_index("seq").astype(jnp.int32)
        me_dp = lax.axis_index("dp").astype(jnp.int32)

        kv = jnp.concatenate([keys_in[0], input_values[0]], axis=-1)
        kv_parts = gather_all(kv)

        sib = siblings[0]
        rel = jnp.bitwise_xor(sib // own, me)
        idx = ((rel % inner) * OUTER + rel // inner) * own + sib % own
        query_grad, terms = attention(idx, queries[0], grad_out[0], kv_parts)

        width = summary.shape[3] // (n_dp * n_seq)
        hidden = summary[0].reshape(own * pos, n_dp, n_seq, width)
        columns = lax.all_to_all(
            jnp.transpose(hidden, (2, 1, 0, 3)), "seq", split_axis=0, concat_axis=0, tiled=True
        )

        near = add_split([terms[0]] + [seq_swap(terms[k], k) for k in range(1, inner)], OUTER)
        mine = add_split(
            [near[0]] + [seq_swap(near[k], k * inner) for k in range(1, OUTER)], 1
        )[0]
        grads = gather_all(mine.reshape(own * pos, 2 * kvw))

        dps = jnp.bitwise_xor(jnp.arange(n_dp, dtype=jnp.int32), me_dp)
        order = jnp.array(
            [o * inner + i for i in range(inner) for o in range(OUTER)], dtype=jnp.int32
        )
        place = jnp.concatenate([me[None], dps, jnp.bitwise_xor(order, me)])
        parts = weight_parts(place, columns, grads, kv_heads)
        total = parts[0]
        for k in range(1, n_dp):
            total = total + swap(parts[k], "dp", n_dp, k)
        return query_grad[None], total

    return per_device


def solution(mesh):
    rows = P("dp", "seq", None, None)
    return jax.shard_map(
        make_per_device(mesh.shape["seq"], mesh.shape["dp"]),
        mesh=mesh,
        in_specs=(P("dp", "seq", None), rows, rows, rows, rows, rows),
        out_specs=(rows, P(("dp", "seq"), None)),
        check_vma=False,
    )
```

```python
import math

import jax
import jax.numpy as jnp
from jax import lax
from jax.experimental import pallas as pl
from jax.experimental.pallas import tpu as pltpu
from jax.sharding import PartitionSpec as P


HEAD = 128
OUTER = 4
VMEM_LIMIT = 28 << 20
CHUNKS = (4,)
F32 = jnp.float32
BF16 = jnp.bfloat16


def dg(a, b, ca, cb):
    return lax.dot_general(a, b, (((ca,), (cb,)), ((), ())), preferred_element_type=F32)


def attention(siblings, me, queries, grad_out, kv_parts, pos, first, heads, kv_heads, before):
    own, length, width = queries.shape
    inner = len(kv_parts) // 2
    sizes = [part.shape[0] for part in kv_parts]
    starts = [sum(sizes[:i]) for i in range(2 * inner)]
    total = sum(sizes)
    kvw2 = kv_parts[0].shape[1]
    group = width // (kv_heads * HEAD)
    span = group * HEAD
    sib = siblings.shape[1]
    rows = sib * pos
    scale = 1.0 / math.sqrt(HEAD)
    scale2 = scale * math.log2(math.e)
    chunk = 128

    def kern(sib_ref, me_ref, q_hbm, g_hbm, *refs):
        kv_in = refs[: 2 * inner]
        refs = refs[2 * inner + (before is not None) :]
        dq_hbm = refs[0]
        outs = refs[1 : 2 * inner + 1]
        kv_s, k_s, v_s, acc, q_buf, g_buf, d_buf, idx_ref, in_sem, out_sem = refs[
            2 * inner + 1 :
        ]
        items = [(c, h) for c in range(own) for h in range(group)]

        def fetches(g, slot, c, h):
            at = pl.ds(pl.multiple_of(((first + g) * group + h) * HEAD, HEAD), HEAD)
            to = slice(h * HEAD, (h + 1) * HEAD)
            return [
                pltpu.make_async_copy(
                    src.at[c, :, at], buf.at[slot, c, :, to], in_sem.at[slot, c, h, n]
                )
                for n, (src, buf) in enumerate(((q_hbm, q_buf), (g_hbm, g_buf)))
            ]

        def store(g, slot, c, h):
            at = pl.ds(pl.multiple_of(((first + g) * group + h) * HEAD, HEAD), HEAD)
            return pltpu.make_async_copy(
                d_buf.at[slot, c, :, h * HEAD : (h + 1) * HEAD],
                dq_hbm.at[c, :, at],
                out_sem.at[slot, c, h],
            )

        for c, h in items:
            for copy in fetches(0, 0, c, h):
                copy.start()
        for c in range(own):
            for j in range(sib):
                which = sib_ref[c, j]
                rel = jnp.bitwise_xor(lax.div(which, own), me_ref[0])
                block = (lax.rem(rel, inner) * OUTER + lax.div(rel, inner)) * own
                idx_ref[c, j] = (block + lax.rem(which, own)) * pos
        for i in range(2 * inner):
            kv_s[starts[i] : starts[i] + sizes[i], :] = kv_in[i][...]

        @pl.loop(0, heads)
        def _(g):
            slot = lax.rem(g, 2)

            @pl.when(g + 1 < heads)
            def _():
                for c, h in items:
                    for copy in fetches(g + 1, 1 - slot, c, h):
                        copy.start()

            k_at = pl.ds(pl.multiple_of(g * HEAD, HEAD), HEAD)
            v_at = pl.ds(pl.multiple_of((heads + g) * HEAD, HEAD), HEAD)
            for c in range(own):
                for j in range(sib):
                    b = pl.ds(pl.multiple_of(idx_ref[c, j], pos), pos)
                    k_s[c, j * pos : (j + 1) * pos, :] = kv_s[b, k_at]
                    v_s[c, j * pos : (j + 1) * pos, :] = kv_s[b, v_at]
            acc[...] = jnp.zeros_like(acc)

            for c, h in items:
                for copy in fetches(g, slot, c, h):
                    copy.wait()

            @pl.when(g >= 2)
            def _():
                for c, h in items:
                    store(g - 2, slot, c, h).wait()

            at = [slice(h * HEAD, (h + 1) * HEAD) for h in range(group)]
            held = {}
            sums = {}

            def scores(n):
                c, h = items[n]
                held[n] = (
                    dg(k_s[c], q_buf[slot, c, :, at[h]], 1, 1),
                    dg(v_s[c], g_buf[slot, c, :, at[h]], 1, 1),
                )

            def soften(n):
                probs = []
                grads = []
                for w in range(0, length, chunk):
                    s = held[n][0][:, w : w + chunk]
                    dp = held[n][1][:, w : w + chunk]
                    m = jnp.max(s, axis=0, keepdims=True)
                    e = jnp.exp2(s * scale2 - m * scale2)
                    p = e * (1.0 / jnp.sum(e, axis=0, keepdims=True))
                    ph = p.astype(BF16)
                    delta = jnp.sum(ph.astype(F32) * dp, axis=0, keepdims=True)
                    grads.append((p * (dp - delta)).astype(BF16))
                    probs.append(ph)
                held[n] = (jnp.concatenate(probs, axis=1), jnp.concatenate(grads, axis=1))

            def products(n):
                c, h = items[n]
                ph, sh = held.pop(n)
                d_buf[slot, c, :, at[h]] = (dg(sh, k_s[c], 0, 0) * scale).astype(BF16)
                dk = dg(sh, q_buf[slot, c, :, at[h]], 1, 0)
                dv = dg(ph, g_buf[slot, c, :, at[h]], 1, 0)
                if h:
                    dk = sums[c][0] + dk
                    dv = sums[c][1] + dv
                sums[c] = (dk, dv)
                if h == group - 1:
                    for j in range(sib):
                        b = pl.ds(pl.multiple_of(idx_ref[c, j], pos), pos)
                        acc[b, :HEAD] += dk[j * pos : (j + 1) * pos, :] * scale
                        acc[b, HEAD:] += dv[j * pos : (j + 1) * pos, :]

            scores(0)
            for n in range(len(items)):
                if n:
                    products(n - 1)
                if n + 1 < len(items):
                    scores(n + 1)
                soften(n)
            products(len(items) - 1)
            for c, h in items:
                store(g, slot, c, h).start()
            o_at = pl.ds(pl.multiple_of(g * 2 * HEAD, 2 * HEAD), 2 * HEAD)
            for i in range(2 * inner):
                outs[i][:, o_at] = acc[starts[i] : starts[i] + sizes[i], :].astype(BF16)

        for g in range(max(heads - 2, 0), heads):
            for c, h in items:
                store(g, g % 2, c, h).wait()

    vmem = pl.BlockSpec(memory_space=pltpu.VMEM)
    hbm = pl.BlockSpec(memory_space=pl.ANY)
    smem = pl.BlockSpec(memory_space=pltpu.SMEM)
    flops = 20 * own * length * group * heads * rows * HEAD
    queries = pltpu.with_memory_space_constraint(queries, pltpu.HBM)
    grad_out = pltpu.with_memory_space_constraint(grad_out, pltpu.HBM)
    args = [siblings, me, queries, grad_out, *kv_parts] + ([before] if before is not None else [])
    res = pl.pallas_call(
        kern,
        in_specs=[smem, smem, hbm, hbm]
        + [vmem] * (2 * inner)
        + ([hbm] if before is not None else []),
        out_specs=[hbm] + [vmem] * (2 * inner),
        scratch_shapes=[
            pltpu.VMEM((total, kvw2), BF16),
            pltpu.VMEM((own, rows, HEAD), BF16),
            pltpu.VMEM((own, rows, HEAD), BF16),
            pltpu.VMEM((total, 2 * HEAD), F32),
            pltpu.VMEM((2, own, length, span), BF16),
            pltpu.VMEM((2, own, length, span), BF16),
            pltpu.VMEM((2, own, length, span), BF16),
            pltpu.SMEM((own, sib), jnp.int32),
            pltpu.SemaphoreType.DMA((2, own, group, 2)),
            pltpu.SemaphoreType.DMA((2, own, group)),
        ],
        out_shape=[jax.ShapeDtypeStruct(queries.shape, BF16)]
        + [jax.ShapeDtypeStruct((size, kvw2), BF16) for size in sizes],
        input_output_aliases={4 + 2 * inner: 0} if before is not None else {},
        compiler_params=pltpu.CompilerParams(vmem_limit_bytes=VMEM_LIMIT),
        cost_estimate=pl.CostEstimate(
            flops=flops, bytes_accessed=6 * queries.size, transcendentals=0
        ),
        name="attention",
    )(*args)
    return res[0], res[1:]


def add_split(parts, pieces):
    shape = parts[0].shape
    each = shape[0] // pieces
    count = len(parts)

    def kern(*refs):
        for i in range(pieces):
            at = slice(i * each, (i + 1) * each)
            total = refs[0][at].astype(F32)
            for r in refs[1:count]:
                total = total + r[at].astype(F32)
            refs[count + i][...] = total.astype(BF16)

    vmem = pl.BlockSpec(memory_space=pltpu.VMEM)
    return pl.pallas_call(
        kern,
        in_specs=[vmem] * count,
        out_specs=[vmem] * pieces,
        out_shape=[jax.ShapeDtypeStruct((each,) + shape[1:], BF16)] * pieces,
        cost_estimate=pl.CostEstimate(
            flops=0, bytes_accessed=2 * count * parts[0].size, transcendentals=0
        ),
        compiler_params=pltpu.CompilerParams(vmem_limit_bytes=8 << 20),
        name="add_split",
    )(*parts)


def weight_parts(place, columns, grads, heads_of, kv_heads):
    devices, dps, rows, width = columns.shape
    chunks = len(grads)
    parts_of = len(grads[0])
    inner = parts_of // 2
    sizes = [part.shape[0] for part in grads[0]]
    starts = [sum(sizes[:i]) for i in range(parts_of)]
    kvw2 = 2 * kv_heads * HEAD

    def kern(place_ref, c_ref, *refs):
        g_in = [refs[i * parts_of : (i + 1) * parts_of] for i in range(chunks)]
        outs = refs[chunks * parts_of : chunks * parts_of + dps]
        g_s, c_s = refs[chunks * parts_of + dps :]
        col = 0
        for n in range(chunks):
            wide = 2 * heads_of[n] * HEAD
            for i in range(parts_of):
                g_s[starts[i] : starts[i] + sizes[i], col : col + wide] = g_in[n][i][...]
            col += wide
        for k in range(dps):
            which = place_ref[k]
            for i in range(inner):
                for o in range(OUTER):
                    at = (i * OUTER + o) * rows
                    c_s[at : at + rows, :] = c_ref[place_ref[dps + i * OUTER + o], which]
            both = dg(c_s[...], g_s[...], 0, 0)
            for h in range(kv_heads):
                lo = 2 * h * HEAD
                outs[k][:, h * HEAD : (h + 1) * HEAD] = both[:, lo : lo + HEAD]
                outs[k][:, (kv_heads + h) * HEAD : (kv_heads + h + 1) * HEAD] = both[
                    :, lo + HEAD : lo + 2 * HEAD
                ]

    vmem = pl.BlockSpec(memory_space=pltpu.VMEM)
    return pl.pallas_call(
        kern,
        in_specs=[pl.BlockSpec(memory_space=pltpu.SMEM)] + [vmem] * (1 + chunks * parts_of),
        out_specs=[vmem] * dps,
        out_shape=[jax.ShapeDtypeStruct((width, kvw2), F32)] * dps,
        scratch_shapes=[
            pltpu.VMEM((devices * rows, kvw2), BF16),
            pltpu.VMEM((devices * rows, width), BF16),
        ],
        compiler_params=pltpu.CompilerParams(vmem_limit_bytes=32 << 20),
        name="weight_parts",
    )(place, columns, *[g for part in grads for g in part])


def make_per_device(n_seq, n_dp):
    inner = n_seq // OUTER

    def swap(x, axis, count, by):
        return lax.ppermute(x, axis, [(i, i ^ by) for i in range(count)])

    def seq_swap(x, by):
        return swap(x, "seq", n_seq, by)

    def gather_all(x):
        rest = [seq_swap(x, k * inner) for k in range(1, OUTER)]
        ones = [x] + [seq_swap(x, k) for k in range(1, inner)]
        rest = jnp.concatenate(rest, axis=0)
        rests = [rest] + [seq_swap(rest, k) for k in range(1, inner)]
        return [part for pair in zip(ones, rests, strict=True) for part in pair]

    def per_device(siblings, queries, grad_out, keys_in, input_values, summary):
        own, pos, kvw = keys_in.shape[1:]
        kv_heads = kvw // HEAD
        me = lax.axis_index("seq").astype(jnp.int32)
        me_dp = lax.axis_index("dp").astype(jnp.int32)

        width = summary.shape[3] // (n_dp * n_seq)
        hidden = summary[0].reshape(own * pos, n_dp, n_seq, width)
        hidden = jnp.transpose(hidden, (2, 1, 0, 3))
        columns = lax.all_to_all(hidden, "seq", split_axis=0, concat_axis=0, tiled=True)

        kv_parts = []
        first = 0
        for heads in CHUNKS:
            at = slice(first * HEAD, (first + heads) * HEAD)
            kv_parts.append(
                gather_all(
                    jnp.concatenate(
                        [keys_in[0, :, :, at], input_values[0, :, :, at]], axis=-1
                    ).reshape(own * pos, 2 * heads * HEAD)
                )
            )
            first += heads

        query_grad = None
        grads = []
        first = 0
        for n, heads in enumerate(CHUNKS):
            query_grad, terms = attention(
                siblings[0],
                me[None],
                queries[0],
                grad_out[0],
                 kv_parts[n], pos, first, heads, kv_heads, query_grad
            )
            first += heads
            ones, rests = terms[::2], terms[1::2]
            near = add_split(
                [rests[0]] + [seq_swap(rests[k], k) for k in range(1, inner)], OUTER - 1
            )
            mine = add_split(
                [ones[0]]
                + [seq_swap(ones[k], k) for k in range(1, inner)]
                + [seq_swap(near[k - 1], k * inner) for k in range(1, OUTER)],
                1,
            )[0]
            grads.append(gather_all(mine))

        dps = jnp.bitwise_xor(jnp.arange(n_dp, dtype=jnp.int32), me_dp)
        order = jnp.array(
            [o * inner + i for i in range(inner) for o in range(OUTER)], dtype=jnp.int32
        )
        place = jnp.concatenate([dps, jnp.bitwise_xor(order, me)])
        parts = weight_parts(place, columns, grads, CHUNKS, kv_heads)
        total = parts[0]
        for k in range(1, n_dp):
            total = total + swap(parts[k], "dp", n_dp, k)
        return query_grad[None], total

    return per_device


def solution(mesh):
    rows = P("dp", "seq", None, None)
    return jax.shard_map(
        make_per_device(mesh.shape["seq"], mesh.shape["dp"]),
        mesh=mesh,
        in_specs=(P("dp", "seq", None), rows, rows, rows, rows, rows),
        out_specs=(rows, P(("dp", "seq"), None)),
        check_vma=False,
    )
```

```python
import math

import jax
import jax.numpy as jnp
from jax import lax
from jax.experimental import pallas as pl
from jax.experimental.pallas import tpu as pltpu
from jax.sharding import PartitionSpec as P


HEAD = 128
OUTER = 4
VMEM_LIMIT = 28 << 20
CHUNKS = (4,)
F32 = jnp.float32
BF16 = jnp.bfloat16


def dg(a, b, ca, cb):
    return lax.dot_general(a, b, (((ca,), (cb,)), ((), ())), preferred_element_type=F32)


def attention(siblings, me, queries, grad_out, kv_parts, pos, first, heads, kv_heads, before):
    own, length, width = queries.shape
    inner = len(kv_parts) // 2
    sizes = [part.shape[0] for part in kv_parts]
    starts = [sum(sizes[:i]) for i in range(2 * inner)]
    total = sum(sizes)
    kvw2 = kv_parts[0].shape[1]
    group = width // (kv_heads * HEAD)
    span = group * HEAD
    sib = siblings.shape[1]
    rows = sib * pos
    scale = 1.0 / math.sqrt(HEAD)
    scale2 = scale * math.log2(math.e)

    def kern(sib_hbm, me_ref, q_hbm, g_hbm, *refs):
        kv_in = refs[: 2 * inner]
        refs = refs[2 * inner + (before is not None) :]
        dq_hbm = refs[0]
        outs = refs[1 : 2 * inner + 1]
        kv_s, k_s, v_s, acc, q_buf, g_buf, d_buf, sib_ref, idx_ref, sib_sem, in_sem, out_sem = refs[
            2 * inner + 1 :
        ]
        items = [(c, h) for c in range(own) for h in range(group)]

        def fetches(g, slot, c, h):
            at = pl.ds(pl.multiple_of(((first + g) * group + h) * HEAD, HEAD), HEAD)
            to = slice(h * HEAD, (h + 1) * HEAD)
            return [
                pltpu.make_async_copy(
                    src.at[c, :, at], buf.at[slot, c, :, to], in_sem.at[slot, c, h, n]
                )
                for n, (src, buf) in enumerate(((q_hbm, q_buf), (g_hbm, g_buf)))
            ]

        def store(g, slot, c, h):
            at = pl.ds(pl.multiple_of(((first + g) * group + h) * HEAD, HEAD), HEAD)
            return pltpu.make_async_copy(
                d_buf.at[slot, c, :, h * HEAD : (h + 1) * HEAD],
                dq_hbm.at[c, :, at],
                out_sem.at[slot, c, h],
            )

        lists = pltpu.make_async_copy(sib_hbm, sib_ref, sib_sem)
        lists.start()
        for c, h in items:
            for copy in fetches(0, 0, c, h):
                copy.start()
        for i in range(2 * inner):
            kv_s[starts[i] : starts[i] + sizes[i], :] = kv_in[i][...]
        lists.wait()
        for c in range(own):
            for j in range(sib):
                which = sib_ref[c, j]
                rel = jnp.bitwise_xor(lax.div(which, own), me_ref[0])
                block = (lax.rem(rel, inner) * OUTER + lax.div(rel, inner)) * own
                idx_ref[c, j] = (block + lax.rem(which, own)) * pos

        @pl.loop(0, heads)
        def _(g):
            slot = lax.rem(g, 2)

            @pl.when(g + 1 < heads)
            def _():
                for c, h in items:
                    for copy in fetches(g + 1, 1 - slot, c, h):
                        copy.start()

            k_at = pl.ds(pl.multiple_of(g * HEAD, HEAD), HEAD)
            v_at = pl.ds(pl.multiple_of((heads + g) * HEAD, HEAD), HEAD)
            for c in range(own):
                for j in range(sib):
                    b = pl.ds(pl.multiple_of(idx_ref[c, j], pos), pos)
                    k_s[c, j * pos : (j + 1) * pos, :] = kv_s[b, k_at]
                    v_s[c, j * pos : (j + 1) * pos, :] = kv_s[b, v_at]
            acc[...] = jnp.zeros_like(acc)

            for c, h in items:
                for copy in fetches(g, slot, c, h):
                    copy.wait()

            @pl.when(g >= 2)
            def _():
                for c, h in items:
                    store(g - 2, slot, c, h).wait()

            at = [slice(h * HEAD, (h + 1) * HEAD) for h in range(group)]
            held = {}
            sums = {}

            def scores(n, w, wide):
                c, h = items[n]
                held.setdefault(n, []).append(
                    (
                        dg(k_s[c], q_buf[slot, c, w : w + wide, at[h]], 1, 1),
                        dg(v_s[c], g_buf[slot, c, w : w + wide, at[h]], 1, 1),
                    )
                )

            def soften(part, out):
                for w in range(0, part[0].shape[1], 128):
                    s = part[0][:, w : w + 128]
                    dp = part[1][:, w : w + 128]
                    m = jnp.max(s, axis=0, keepdims=True)
                    e = jnp.exp2(s * scale2 - m * scale2)
                    p = e * (1.0 / jnp.sum(e, axis=0, keepdims=True))
                    ph = p.astype(BF16)
                    delta = jnp.sum(ph.astype(F32) * dp, axis=0, keepdims=True)
                    out.append((ph, (p * (dp - delta)).astype(BF16)))

            def query_part(n):
                c, h = items[n]
                d_buf[slot, c, :, at[h]] = (dg(held[n][1], k_s[c], 0, 0) * scale).astype(BF16)

            def key_part(n, which):
                c, h = items[n]
                src = g_buf if which else q_buf
                d = dg(src[slot, c, :, at[h]].T, held[n][1 - which], 1, 1)
                if h:
                    d = sums[c, which] + d
                sums[c, which] = d
                if h == group - 1:
                    d = d.T
                    for j in range(sib):
                        b = pl.ds(pl.multiple_of(idx_ref[c, j], pos), pos)
                        if which:
                            acc[b, HEAD:] += d[j * pos : (j + 1) * pos, :]
                        else:
                            acc[b, :HEAD] += d[j * pos : (j + 1) * pos, :] * scale

            count = len(items)
            wide = length // 2
            for w in range(2):
                scores(0, w * wide, wide)
            for n in range(count + 1):
                work = []
                if n:
                    work += [
                        (query_part, (n - 1,)), (key_part, (n - 1, 0)), (key_part, (n - 1, 1))
                    ]
                if n + 1 < count:
                    work += [(scores, (n + 1, w * wide, wide)) for w in range(2)]
                soft = list(held[n]) if n < count else []
                out = []
                step = -(-len(work) // max(1, len(soft)))
                while work or soft:
                    for f, a in work[:step]:
                        f(*a)
                    work = work[step:]
                    if soft:
                        soften(soft.pop(0), out)
                if n < count:
                    held[n] = [jnp.concatenate([o[i] for o in out], axis=1) for i in (0, 1)]
            for c, h in items:
                store(g, slot, c, h).start()
            o_at = pl.ds(pl.multiple_of(g * 2 * HEAD, 2 * HEAD), 2 * HEAD)
            for i in range(2 * inner):
                outs[i][:, o_at] = acc[starts[i] : starts[i] + sizes[i], :].astype(BF16)

        for g in range(max(heads - 2, 0), heads):
            for c, h in items:
                store(g, g % 2, c, h).wait()

    vmem = pl.BlockSpec(memory_space=pltpu.VMEM)
    hbm = pl.BlockSpec(memory_space=pl.ANY)
    smem = pl.BlockSpec(memory_space=pltpu.SMEM)
    flops = 20 * own * length * group * heads * rows * HEAD
    siblings = pltpu.with_memory_space_constraint(siblings, pltpu.HBM)
    queries = pltpu.with_memory_space_constraint(queries, pltpu.HBM)
    grad_out = pltpu.with_memory_space_constraint(grad_out, pltpu.HBM)
    args = [siblings, me, queries, grad_out, *kv_parts] + ([before] if before is not None else [])
    res = pl.pallas_call(
        kern,
        in_specs=[hbm, smem, hbm, hbm]
        + [vmem] * (2 * inner)
        + ([hbm] if before is not None else []),
        out_specs=[hbm] + [vmem] * (2 * inner),
        scratch_shapes=[
            pltpu.VMEM((total, kvw2), BF16),
            pltpu.VMEM((own, rows, HEAD), BF16),
            pltpu.VMEM((own, rows, HEAD), BF16),
            pltpu.VMEM((total, 2 * HEAD), F32),
            pltpu.VMEM((2, own, length, span), BF16),
            pltpu.VMEM((2, own, length, span), BF16),
            pltpu.VMEM((2, own, length, span), BF16),
            pltpu.SMEM((own, sib), jnp.int32),
            pltpu.SMEM((own, sib), jnp.int32),
            pltpu.SemaphoreType.DMA(()),
            pltpu.SemaphoreType.DMA((2, own, group, 2)),
            pltpu.SemaphoreType.DMA((2, own, group)),
        ],
        out_shape=[jax.ShapeDtypeStruct(queries.shape, BF16)]
        + [jax.ShapeDtypeStruct((size, kvw2), BF16) for size in sizes],
        input_output_aliases={4 + 2 * inner: 0} if before is not None else {},
        compiler_params=pltpu.CompilerParams(vmem_limit_bytes=VMEM_LIMIT),
        cost_estimate=pl.CostEstimate(
            flops=flops, bytes_accessed=6 * queries.size, transcendentals=0
        ),
        name="attention",
    )(*args)
    return res[0], res[1:]


def add_split(parts, pieces):
    shape = parts[0].shape
    each = shape[0] // pieces
    count = len(parts)

    def kern(*refs):
        for i in range(pieces):
            at = slice(i * each, (i + 1) * each)
            total = refs[0][at].astype(F32)
            for r in refs[1:count]:
                total = total + r[at].astype(F32)
            refs[count + i][...] = total.astype(BF16)

    vmem = pl.BlockSpec(memory_space=pltpu.VMEM)
    return pl.pallas_call(
        kern,
        in_specs=[vmem] * count,
        out_specs=[vmem] * pieces,
        out_shape=[jax.ShapeDtypeStruct((each,) + shape[1:], BF16)] * pieces,
        cost_estimate=pl.CostEstimate(
            flops=0, bytes_accessed=2 * count * parts[0].size, transcendentals=0
        ),
        compiler_params=pltpu.CompilerParams(vmem_limit_bytes=8 << 20),
        name="add_split",
    )(*parts)


def by_target(hidden, devices, dps):
    rows, total = hidden.shape
    width = total // (devices * dps)

    def kern(h_ref, o_ref):
        for t in range(devices):
            for d in range(dps):
                lo = (d * devices + t) * width
                o_ref[t, :, d * width : (d + 1) * width] = h_ref[:, lo : lo + width]

    vmem = pl.BlockSpec(memory_space=pltpu.VMEM)
    return pl.pallas_call(
        kern,
        in_specs=[vmem],
        out_specs=vmem,
        out_shape=jax.ShapeDtypeStruct((devices, rows, dps * width), BF16),
        compiler_params=pltpu.CompilerParams(vmem_limit_bytes=8 << 20),
        name="by_target",
    )(hidden)


def weight_parts(place, columns, grads, heads_of, kv_heads, dps):
    devices, rows, wide = columns.shape
    width = wide // dps
    chunks = len(grads)
    parts_of = len(grads[0])
    sizes = [part.shape[0] for part in grads[0]]
    starts = [sum(sizes[:i]) for i in range(parts_of)]
    kvw2 = 2 * kv_heads * HEAD

    def kern(place_ref, c_ref, *refs):
        g_in = [refs[i * parts_of : (i + 1) * parts_of] for i in range(chunks)]
        outs = refs[chunks * parts_of : chunks * parts_of + dps]
        g_s, c_s, w_s = refs[chunks * parts_of + dps :]
        col = 0
        for n in range(chunks):
            span = 2 * heads_of[n] * HEAD
            for i in range(parts_of):
                g_s[starts[i] : starts[i] + sizes[i], col : col + span] = g_in[n][i][...]
            col += span
        for n in range(devices):
            c_s[n * rows : (n + 1) * rows, :] = c_ref[place_ref[dps + n]]
        w_s[...] = dg(c_s[...], g_s[...], 0, 0)
        for k in range(dps):
            at = pl.ds(pl.multiple_of(place_ref[k] * width, 8), width)
            for h in range(kv_heads):
                lo = 2 * h * HEAD
                outs[k][:, h * HEAD : (h + 1) * HEAD] = w_s[at, lo : lo + HEAD]
                outs[k][:, (kv_heads + h) * HEAD : (kv_heads + h + 1) * HEAD] = w_s[
                    at, lo + HEAD : lo + 2 * HEAD
                ]

    vmem = pl.BlockSpec(memory_space=pltpu.VMEM)
    return pl.pallas_call(
        kern,
        in_specs=[pl.BlockSpec(memory_space=pltpu.SMEM)] + [vmem] * (1 + chunks * parts_of),
        out_specs=[vmem] * dps,
        out_shape=[jax.ShapeDtypeStruct((width, kvw2), F32)] * dps,
        scratch_shapes=[
            pltpu.VMEM((devices * rows, kvw2), BF16),
            pltpu.VMEM((devices * rows, wide), BF16),
            pltpu.VMEM((wide, kvw2), F32),
        ],
        compiler_params=pltpu.CompilerParams(vmem_limit_bytes=32 << 20),
        name="weight_parts",
    )(place, columns, *[g for part in grads for g in part])


def make_per_device(n_seq, n_dp):
    inner = n_seq // OUTER

    def swap(x, axis, count, by):
        return lax.ppermute(x, axis, [(i, i ^ by) for i in range(count)])

    def seq_swap(x, by):
        return swap(x, "seq", n_seq, by)

    def gather_all(x):
        rest = [seq_swap(x, k * inner) for k in range(1, OUTER)]
        ones = [x] + [seq_swap(x, k) for k in range(1, inner)]
        rest = jnp.concatenate(rest, axis=0)
        rests = [rest] + [seq_swap(rest, k) for k in range(1, inner)]
        return [part for pair in zip(ones, rests, strict=True) for part in pair]

    def per_device(siblings, queries, grad_out, keys_in, input_values, summary):
        own, pos, kvw = keys_in.shape[1:]
        kv_heads = kvw // HEAD
        me = lax.axis_index("seq").astype(jnp.int32)
        me_dp = lax.axis_index("dp").astype(jnp.int32)

        hidden = by_target(summary[0].reshape(own * pos, summary.shape[3]), n_seq, n_dp)
        columns = lax.all_to_all(hidden, "seq", split_axis=0, concat_axis=0, tiled=True)

        kv_parts = []
        first = 0
        for heads in CHUNKS:
            at = slice(first * HEAD, (first + heads) * HEAD)
            kv_parts.append(
                gather_all(
                    jnp.concatenate(
                        [keys_in[0, :, :, at], input_values[0, :, :, at]], axis=-1
                    ).reshape(own * pos, 2 * heads * HEAD)
                )
            )
            first += heads

        query_grad = None
        grads = []
        first = 0
        for n, heads in enumerate(CHUNKS):
            query_grad, terms = attention(
                siblings[0],
                me[None],
                queries[0],
                grad_out[0],
                 kv_parts[n], pos, first, heads, kv_heads, query_grad
            )
            first += heads
            ones, rests = terms[::2], terms[1::2]
            near = add_split(
                [rests[0]] + [seq_swap(rests[k], k) for k in range(1, inner)], OUTER - 1
            )
            mine = add_split(
                [ones[0]]
                + [seq_swap(ones[k], k) for k in range(1, inner)]
                + [seq_swap(near[k - 1], k * inner) for k in range(1, OUTER)],
                1,
            )[0]
            grads.append(gather_all(mine))

        dps = jnp.bitwise_xor(jnp.arange(n_dp, dtype=jnp.int32), me_dp)
        order = jnp.array(
            [o * inner + i for i in range(inner) for o in range(OUTER)], dtype=jnp.int32
        )
        place = jnp.concatenate([dps, jnp.bitwise_xor(order, me)])
        parts = weight_parts(place, columns, grads, CHUNKS, kv_heads, n_dp)
        total = parts[0]
        for k in range(1, n_dp):
            total = total + swap(parts[k], "dp", n_dp, k)
        return query_grad[None], total

    return per_device


def solution(mesh):
    rows = P("dp", "seq", None, None)
    return jax.shard_map(
        make_per_device(mesh.shape["seq"], mesh.shape["dp"]),
        mesh=mesh,
        in_specs=(P("dp", "seq", None), rows, rows, rows, rows, rows),
        out_specs=(rows, P(("dp", "seq"), None)),
        check_vma=False,
    )
```

```python
import math

import jax
import jax.numpy as jnp
from jax import lax
from jax.experimental import pallas as pl
from jax.experimental.pallas import tpu as pltpu
from jax.sharding import PartitionSpec as P


HEAD = 128
OUTER = 4
VMEM_LIMIT = 28 << 20
CHUNKS = (4,)
EARLY = {"rows": True, "sum": False, "grads": True}
F32 = jnp.float32
BF16 = jnp.bfloat16


def dg(a, b, ca, cb):
    return lax.dot_general(a, b, (((ca,), (cb,)), ((), ())), preferred_element_type=F32)


def attention(siblings, me, queries, grad_out, kv_parts, sizes_out, pos, first, heads, kv_heads, before):
    own, length, width = queries.shape
    sizes = [part.shape[0] for part in kv_parts]
    starts = [sum(sizes[:i]) for i in range(len(sizes))]
    starts_out = [sum(sizes_out[:i]) for i in range(len(sizes_out))]
    total = sum(sizes)
    inner = total // (OUTER * queries.shape[0] * pos)
    kvw2 = kv_parts[0].shape[1]
    group = width // (kv_heads * HEAD)
    span = group * HEAD
    sib = siblings.shape[1]
    rows = sib * pos
    scale = 1.0 / math.sqrt(HEAD)
    scale2 = scale * math.log2(math.e)

    def kern(sib_hbm, me_ref, q_hbm, g_hbm, *refs):
        kv_in = refs[: len(sizes)]
        refs = refs[len(sizes) + (before is not None) :]
        dq_hbm = refs[0]
        outs = refs[1 : len(sizes_out) + 1]
        kv_s, k_s, v_s, acc, q_buf, g_buf, d_buf, sib_ref, idx_ref, sib_sem, in_sem, out_sem = refs[
            len(sizes_out) + 1 :
        ]
        items = [(c, h) for c in range(own) for h in range(group)]

        def fetches(g, slot, c, h):
            at = pl.ds(pl.multiple_of(((first + g) * group + h) * HEAD, HEAD), HEAD)
            to = slice(h * HEAD, (h + 1) * HEAD)
            return [
                pltpu.make_async_copy(
                    src.at[c, :, at], buf.at[slot, c, :, to], in_sem.at[slot, c, h, n]
                )
                for n, (src, buf) in enumerate(((q_hbm, q_buf), (g_hbm, g_buf)))
            ]

        def store(g, slot, c, h):
            at = pl.ds(pl.multiple_of(((first + g) * group + h) * HEAD, HEAD), HEAD)
            return pltpu.make_async_copy(
                d_buf.at[slot, c, :, h * HEAD : (h + 1) * HEAD],
                dq_hbm.at[c, :, at],
                out_sem.at[slot, c, h],
            )

        lists = pltpu.make_async_copy(sib_hbm, sib_ref, sib_sem)
        lists.start()
        for c, h in items:
            for copy in fetches(0, 0, c, h):
                copy.start()
        for i in range(len(sizes)):
            kv_s[starts[i] : starts[i] + sizes[i], :] = kv_in[i][...]
        lists.wait()
        for c in range(own):
            for j in range(sib):
                which = sib_ref[c, j]
                rel = jnp.bitwise_xor(lax.div(which, own), me_ref[0])
                block = (lax.rem(rel, inner) * OUTER + lax.div(rel, inner)) * own
                idx_ref[c, j] = (block + lax.rem(which, own)) * pos

        @pl.loop(0, heads)
        def _(g):
            slot = lax.rem(g, 2)

            @pl.when(g + 1 < heads)
            def _():
                for c, h in items:
                    for copy in fetches(g + 1, 1 - slot, c, h):
                        copy.start()

            k_at = pl.ds(pl.multiple_of(g * HEAD, HEAD), HEAD)
            v_at = pl.ds(pl.multiple_of((heads + g) * HEAD, HEAD), HEAD)
            for c in range(own):
                for j in range(sib):
                    b = pl.ds(pl.multiple_of(idx_ref[c, j], pos), pos)
                    k_s[c, j * pos : (j + 1) * pos, :] = kv_s[b, k_at]
                    v_s[c, j * pos : (j + 1) * pos, :] = kv_s[b, v_at]
            acc[...] = jnp.zeros_like(acc)

            for c, h in items:
                for copy in fetches(g, slot, c, h):
                    copy.wait()

            @pl.when(g >= 2)
            def _():
                for c, h in items:
                    store(g - 2, slot, c, h).wait()

            at = [slice(h * HEAD, (h + 1) * HEAD) for h in range(group)]
            held = {}
            sums = {}

            def scores(n, w, wide):
                c, h = items[n]
                held.setdefault(n, []).append(
                    (
                        dg(k_s[c], q_buf[slot, c, w : w + wide, at[h]], 1, 1),
                        dg(v_s[c], g_buf[slot, c, w : w + wide, at[h]], 1, 1),
                    )
                )

            def soften(part, out):
                for w in range(0, part[0].shape[1], 128):
                    s = part[0][:, w : w + 128]
                    dp = part[1][:, w : w + 128]
                    m = jnp.max(s, axis=0, keepdims=True)
                    e = jnp.exp2(s * scale2 - m * scale2)
                    p = e * (1.0 / jnp.sum(e, axis=0, keepdims=True))
                    ph = p.astype(BF16)
                    delta = jnp.sum(ph.astype(F32) * dp, axis=0, keepdims=True)
                    out.append((ph, (p * (dp - delta)).astype(BF16)))

            def query_part(n):
                c, h = items[n]
                d_buf[slot, c, :, at[h]] = (dg(held[n][1], k_s[c], 0, 0) * scale).astype(BF16)

            def key_part(n, which):
                c, h = items[n]
                src = g_buf if which else q_buf
                d = dg(src[slot, c, :, at[h]].T, held[n][1 - which], 1, 1)
                if h:
                    d = sums[c, which] + d
                sums[c, which] = d
                if h == group - 1:
                    d = d.T
                    for j in range(sib):
                        b = pl.ds(pl.multiple_of(idx_ref[c, j], pos), pos)
                        if which:
                            acc[b, HEAD:] += d[j * pos : (j + 1) * pos, :]
                        else:
                            acc[b, :HEAD] += d[j * pos : (j + 1) * pos, :] * scale

            count = len(items)
            wide = length // 2
            for w in range(2):
                scores(0, w * wide, wide)
            for n in range(count + 1):
                work = []
                if n:
                    work += [
                        (query_part, (n - 1,)), (key_part, (n - 1, 0)), (key_part, (n - 1, 1))
                    ]
                if n + 1 < count:
                    work += [(scores, (n + 1, w * wide, wide)) for w in range(2)]
                soft = list(held[n]) if n < count else []
                out = []
                step = -(-len(work) // max(1, len(soft)))
                while work or soft:
                    for f, a in work[:step]:
                        f(*a)
                    work = work[step:]
                    if soft:
                        soften(soft.pop(0), out)
                if n and items[n - 1][1] == group - 1:
                    for one in range(group):
                        store(g, slot, items[n - 1][0], one).start()
                if n < count:
                    held[n] = [jnp.concatenate([o[i] for o in out], axis=1) for i in (0, 1)]
            o_at = pl.ds(pl.multiple_of(g * 2 * HEAD, 2 * HEAD), 2 * HEAD)
            for i in range(len(sizes_out)):
                outs[i][:, o_at] = acc[
                    starts_out[i] : starts_out[i] + sizes_out[i], :
                ].astype(BF16)

        for g in range(max(heads - 2, 0), heads):
            for c, h in items:
                store(g, g % 2, c, h).wait()

    vmem = pl.BlockSpec(memory_space=pltpu.VMEM)
    hbm = pl.BlockSpec(memory_space=pl.ANY)
    smem = pl.BlockSpec(memory_space=pltpu.SMEM)
    flops = 20 * own * length * group * heads * rows * HEAD
    siblings = pltpu.with_memory_space_constraint(siblings, pltpu.HBM)
    queries = pltpu.with_memory_space_constraint(queries, pltpu.HBM)
    grad_out = pltpu.with_memory_space_constraint(grad_out, pltpu.HBM)
    args = [siblings, me, queries, grad_out, *kv_parts] + ([before] if before is not None else [])
    res = pl.pallas_call(
        kern,
        in_specs=[hbm, smem, hbm, hbm]
        + [vmem] * len(sizes)
        + ([hbm] if before is not None else []),
        out_specs=[hbm] + [vmem] * len(sizes_out),
        scratch_shapes=[
            pltpu.VMEM((total, kvw2), BF16),
            pltpu.VMEM((own, rows, HEAD), BF16),
            pltpu.VMEM((own, rows, HEAD), BF16),
            pltpu.VMEM((total, 2 * HEAD), F32),
            pltpu.VMEM((2, own, length, span), BF16),
            pltpu.VMEM((2, own, length, span), BF16),
            pltpu.VMEM((2, own, length, span), BF16),
            pltpu.SMEM((own, sib), jnp.int32),
            pltpu.SMEM((own, sib), jnp.int32),
            pltpu.SemaphoreType.DMA(()),
            pltpu.SemaphoreType.DMA((2, own, group, 2)),
            pltpu.SemaphoreType.DMA((2, own, group)),
        ],
        out_shape=[jax.ShapeDtypeStruct(queries.shape, BF16)]
        + [jax.ShapeDtypeStruct((size, kvw2), BF16) for size in sizes_out],
        input_output_aliases={4 + len(sizes): 0} if before is not None else {},
        compiler_params=pltpu.CompilerParams(vmem_limit_bytes=VMEM_LIMIT),
        cost_estimate=pl.CostEstimate(
            flops=flops, bytes_accessed=6 * queries.size, transcendentals=0
        ),
        name="attention",
    )(*args)
    return res[0], res[1:]


def add_split(parts, pieces):
    shape = parts[0].shape
    each = shape[0] // pieces
    count = len(parts)

    def kern(*refs):
        for i in range(pieces):
            at = slice(i * each, (i + 1) * each)
            total = refs[0][at].astype(F32)
            for r in refs[1:count]:
                total = total + r[at].astype(F32)
            refs[count + i][...] = total.astype(BF16)

    vmem = pl.BlockSpec(memory_space=pltpu.VMEM)
    return pl.pallas_call(
        kern,
        in_specs=[vmem] * count,
        out_specs=[vmem] * pieces,
        out_shape=[jax.ShapeDtypeStruct((each,) + shape[1:], BF16)] * pieces,
        cost_estimate=pl.CostEstimate(
            flops=0, bytes_accessed=2 * count * parts[0].size, transcendentals=0
        ),
        compiler_params=pltpu.CompilerParams(vmem_limit_bytes=8 << 20),
        name="add_split",
    )(*parts)


def by_target(hidden, devices, dps):
    rows, total = hidden.shape
    width = total // (devices * dps)

    def kern(h_ref, o_ref):
        for t in range(devices):
            for d in range(dps):
                lo = (d * devices + t) * width
                o_ref[t, :, d * width : (d + 1) * width] = h_ref[:, lo : lo + width]

    vmem = pl.BlockSpec(memory_space=pltpu.VMEM)
    return pl.pallas_call(
        kern,
        in_specs=[vmem],
        out_specs=vmem,
        out_shape=jax.ShapeDtypeStruct((devices, rows, dps * width), BF16),
        compiler_params=pltpu.CompilerParams(vmem_limit_bytes=8 << 20),
        name="by_target",
    )(hidden)


def weight_parts(place, columns, grads, heads_of, kv_heads, dps):
    devices, rows, wide = columns.shape
    width = wide // dps
    chunks = len(grads)
    parts_of = len(grads[0])
    sizes = [part.shape[0] for part in grads[0]]
    starts = [sum(sizes[:i]) for i in range(parts_of)]
    kvw2 = 2 * kv_heads * HEAD

    def kern(place_ref, c_ref, *refs):
        g_in = [refs[i * parts_of : (i + 1) * parts_of] for i in range(chunks)]
        outs = refs[chunks * parts_of : chunks * parts_of + dps]
        g_s, c_s, w_s = refs[chunks * parts_of + dps :]
        col = 0
        for n in range(chunks):
            span = 2 * heads_of[n] * HEAD
            for i in range(parts_of):
                g_s[starts[i] : starts[i] + sizes[i], col : col + span] = g_in[n][i][...]
            col += span
        for n in range(devices):
            c_s[n * rows : (n + 1) * rows, :] = c_ref[place_ref[dps + n]]
        w_s[...] = dg(c_s[...], g_s[...], 0, 0)
        for k in range(dps):
            at = pl.ds(pl.multiple_of(place_ref[k] * width, 8), width)
            for h in range(kv_heads):
                lo = 2 * h * HEAD
                outs[k][:, h * HEAD : (h + 1) * HEAD] = w_s[at, lo : lo + HEAD]
                outs[k][:, (kv_heads + h) * HEAD : (kv_heads + h + 1) * HEAD] = w_s[
                    at, lo + HEAD : lo + 2 * HEAD
                ]

    vmem = pl.BlockSpec(memory_space=pltpu.VMEM)
    return pl.pallas_call(
        kern,
        in_specs=[pl.BlockSpec(memory_space=pltpu.SMEM)] + [vmem] * (1 + chunks * parts_of),
        out_specs=[vmem] * dps,
        out_shape=[jax.ShapeDtypeStruct((width, kvw2), F32)] * dps,
        scratch_shapes=[
            pltpu.VMEM((devices * rows, kvw2), BF16),
            pltpu.VMEM((devices * rows, wide), BF16),
            pltpu.VMEM((wide, kvw2), F32),
        ],
        compiler_params=pltpu.CompilerParams(vmem_limit_bytes=32 << 20),
        name="weight_parts",
    )(place, columns, *[g for part in grads for g in part])


def make_per_device(n_seq, n_dp):
    inner = n_seq // OUTER

    def swap(x, axis, count, by):
        return lax.ppermute(x, axis, [(i, i ^ by) for i in range(count)])

    def seq_swap(x, by):
        return swap(x, "seq", n_seq, by)

    def gather_all(x, early):
        rest = [seq_swap(x, k * inner) for k in range(1, OUTER)]
        if not early:
            rest = jnp.concatenate([x] + rest, axis=0)
            return [rest] + [seq_swap(rest, k) for k in range(1, inner)]
        ones = [x] + [seq_swap(x, k) for k in range(1, inner)]
        rest = jnp.concatenate(rest, axis=0)
        rests = [rest] + [seq_swap(rest, k) for k in range(1, inner)]
        return [part for pair in zip(ones, rests, strict=True) for part in pair]

    def per_device(siblings, queries, grad_out, keys_in, input_values, summary):
        own, pos, kvw = keys_in.shape[1:]
        kv_heads = kvw // HEAD
        me = lax.axis_index("seq").astype(jnp.int32)
        me_dp = lax.axis_index("dp").astype(jnp.int32)

        hidden = by_target(summary[0].reshape(own * pos, summary.shape[3]), n_seq, n_dp)
        columns = lax.all_to_all(hidden, "seq", split_axis=0, concat_axis=0, tiled=True)

        kv_parts = []
        first = 0
        for heads in CHUNKS:
            at = slice(first * HEAD, (first + heads) * HEAD)
            kv_parts.append(
                gather_all(
                    jnp.concatenate(
                        [keys_in[0, :, :, at], input_values[0, :, :, at]], axis=-1
                    ).reshape(own * pos, 2 * heads * HEAD),
                    EARLY["rows"],
                )
            )
            first += heads

        query_grad = None
        grads = []
        first = 0
        for n, heads in enumerate(CHUNKS):
            query_grad, terms = attention(
                siblings[0],
                me[None],
                queries[0],
                grad_out[0],
                 kv_parts[n],
                ([own * pos, (OUTER - 1) * own * pos] if EARLY["sum"] else [OUTER * own * pos])
                * inner,
                pos, first, heads, kv_heads, query_grad
            )
            first += heads
            ones, rests = (terms[::2], terms[1::2]) if EARLY["sum"] else ([], terms)
            near = add_split(
                [rests[0]] + [seq_swap(rests[k], k) for k in range(1, inner)],
                rests[0].shape[0] // (own * pos),
            )
            here = [ones[0]] if EARLY["sum"] else [near[0]]
            here += [seq_swap(ones[k], k) for k in range(1, len(ones))]
            away = near if EARLY["sum"] else near[1:]
            here += [seq_swap(away[k - 1], k * inner) for k in range(1, OUTER)]
            mine = add_split(here, 1)[0]
            grads.append(gather_all(mine, EARLY["grads"]))

        dps = jnp.bitwise_xor(jnp.arange(n_dp, dtype=jnp.int32), me_dp)
        order = jnp.array(
            [o * inner + i for i in range(inner) for o in range(OUTER)], dtype=jnp.int32
        )
        place = jnp.concatenate([dps, jnp.bitwise_xor(order, me)])
        parts = weight_parts(place, columns, grads, CHUNKS, kv_heads, n_dp)
        total = parts[0]
        for k in range(1, n_dp):
            total = total + swap(parts[k], "dp", n_dp, k)
        return query_grad[None], total

    return per_device


def solution(mesh):
    rows = P("dp", "seq", None, None)
    return jax.shard_map(
        make_per_device(mesh.shape["seq"], mesh.shape["dp"]),
        mesh=mesh,
        in_specs=(P("dp", "seq", None), rows, rows, rows, rows, rows),
        out_specs=(rows, P(("dp", "seq"), None)),
        check_vma=False,
    )
```

```python
import math

import jax
import jax.numpy as jnp
from jax import lax
from jax.experimental import pallas as pl
from jax.experimental.pallas import tpu as pltpu
from jax.sharding import PartitionSpec as P


HEAD = 128
OUTER = 4
VMEM_LIMIT = 28 << 20
CHUNKS = (4,)
EARLY = {"rows": True, "sum": False, "grads": True}
F32 = jnp.float32
BF16 = jnp.bfloat16


def dg(a, b, ca, cb):
    return lax.dot_general(a, b, (((ca,), (cb,)), ((), ())), preferred_element_type=F32)


def attention(siblings, me, queries, grad_out, kv_parts, sizes_out, pos, first, heads, kv_heads, before):
    own, length, width = queries.shape
    sizes = [part.shape[0] for part in kv_parts]
    starts = [sum(sizes[:i]) for i in range(len(sizes))]
    starts_out = [sum(sizes_out[:i]) for i in range(len(sizes_out))]
    total = sum(sizes)
    inner = total // (OUTER * queries.shape[0] * pos)
    kvw2 = kv_parts[0].shape[1]
    group = width // (kv_heads * HEAD)
    span = group * HEAD
    sib = siblings.shape[1]
    rows = sib * pos
    scale = 1.0 / math.sqrt(HEAD)
    scale2 = scale * math.log2(math.e)

    def kern(sib_hbm, me_ref, q_hbm, g_hbm, *refs):
        kv_in = refs[: len(sizes)]
        refs = refs[len(sizes) + (before is not None) :]
        dq_hbm = refs[0]
        outs = refs[1 : len(sizes_out) + 1]
        kv_s, k_s, v_s, acc, q_buf, g_buf, d_buf, sib_ref, idx_ref, sib_sem, in_sem, out_sem = refs[
            len(sizes_out) + 1 :
        ]
        items = [(c, h) for c in range(own) for h in range(group)]

        def fetches(g, slot, c, h):
            at = pl.ds(pl.multiple_of(((first + g) * group + h) * HEAD, HEAD), HEAD)
            to = slice(h * HEAD, (h + 1) * HEAD)
            return [
                pltpu.make_async_copy(
                    src.at[c, :, at], buf.at[slot, c, :, to], in_sem.at[slot, c, h, n]
                )
                for n, (src, buf) in enumerate(((q_hbm, q_buf), (g_hbm, g_buf)))
            ]

        def store(g, slot, c, h):
            at = pl.ds(pl.multiple_of(((first + g) * group + h) * HEAD, HEAD), HEAD)
            return pltpu.make_async_copy(
                d_buf.at[slot, c, :, h * HEAD : (h + 1) * HEAD],
                dq_hbm.at[c, :, at],
                out_sem.at[slot, c, h],
            )

        lists = pltpu.make_async_copy(sib_hbm, sib_ref, sib_sem)
        lists.start()
        for c, h in items:
            for copy in fetches(0, 0, c, h):
                copy.start()
        for i in range(len(sizes)):
            kv_s[starts[i] : starts[i] + sizes[i], :] = kv_in[i][...]
        lists.wait()
        for c in range(own):
            for j in range(sib):
                which = sib_ref[c, j]
                rel = jnp.bitwise_xor(lax.div(which, own), me_ref[0])
                block = (lax.rem(rel, inner) * OUTER + lax.div(rel, inner)) * own
                idx_ref[c, j] = (block + lax.rem(which, own)) * pos

        @pl.loop(0, heads)
        def _(g):
            slot = lax.rem(g, 2)

            @pl.when(g + 1 < heads)
            def _():
                for c, h in items:
                    for copy in fetches(g + 1, 1 - slot, c, h):
                        copy.start()

            k_at = pl.ds(pl.multiple_of(g * HEAD, HEAD), HEAD)
            v_at = pl.ds(pl.multiple_of((heads + g) * HEAD, HEAD), HEAD)
            for c in range(own):
                for j in range(sib):
                    b = pl.ds(pl.multiple_of(idx_ref[c, j], pos), pos)
                    k_s[c, j * pos : (j + 1) * pos, :] = kv_s[b, k_at]
                    v_s[c, j * pos : (j + 1) * pos, :] = kv_s[b, v_at]
            acc[...] = jnp.zeros_like(acc)

            for c, h in items:
                for copy in fetches(g, slot, c, h):
                    copy.wait()

            @pl.when(g >= 2)
            def _():
                for c, h in items:
                    store(g - 2, slot, c, h).wait()

            at = [slice(h * HEAD, (h + 1) * HEAD) for h in range(group)]
            held = {}
            sums = {}

            def scores(n, w, wide):
                c, h = items[n]
                held.setdefault(n, []).append(
                    (
                        dg(k_s[c], q_buf[slot, c, w : w + wide, at[h]], 1, 1),
                        dg(v_s[c], g_buf[slot, c, w : w + wide, at[h]], 1, 1),
                    )
                )

            def soften(part, out):
                for w in range(0, part[0].shape[1], 128):
                    s = part[0][:, w : w + 128]
                    dp = part[1][:, w : w + 128]
                    m = jnp.max(s, axis=0, keepdims=True)
                    e = jnp.exp2(s * scale2 - m * scale2)
                    p = e * (1.0 / jnp.sum(e, axis=0, keepdims=True))
                    ph = p.astype(BF16)
                    delta = jnp.sum(ph.astype(F32) * dp, axis=0, keepdims=True)
                    out.append((ph, (p * (dp - delta)).astype(BF16)))

            def query_part(n):
                c, h = items[n]
                d_buf[slot, c, :, at[h]] = (dg(held[n][1], k_s[c], 0, 0) * scale).astype(BF16)

            def key_part(n, which):
                c, h = items[n]
                src = g_buf if which else q_buf
                d = dg(src[slot, c, :, at[h]].T, held[n][1 - which], 1, 1)
                if h:
                    d = sums[c, which] + d
                sums[c, which] = d
                if h == group - 1:
                    d = d.T
                    for j in range(sib):
                        b = pl.ds(pl.multiple_of(idx_ref[c, j], pos), pos)
                        if which:
                            acc[b, HEAD:] += d[j * pos : (j + 1) * pos, :]
                        else:
                            acc[b, :HEAD] += d[j * pos : (j + 1) * pos, :] * scale

            count = len(items)
            wide = length // 2
            for w in range(2):
                scores(0, w * wide, wide)
            for n in range(count + 1):
                work = []
                if n:
                    work += [
                        (query_part, (n - 1,)), (key_part, (n - 1, 0)), (key_part, (n - 1, 1))
                    ]
                if n + 1 < count:
                    work += [(scores, (n + 1, w * wide, wide)) for w in range(2)]
                soft = list(held[n]) if n < count else []
                out = []
                step = -(-len(work) // max(1, len(soft)))
                while work or soft:
                    for f, a in work[:step]:
                        f(*a)
                    work = work[step:]
                    if soft:
                        soften(soft.pop(0), out)
                if n and items[n - 1][1] == group - 1:
                    for one in range(group):
                        store(g, slot, items[n - 1][0], one).start()
                if n < count:
                    held[n] = [jnp.concatenate([o[i] for o in out], axis=1) for i in (0, 1)]
            o_at = pl.ds(pl.multiple_of(g * 2 * HEAD, 2 * HEAD), 2 * HEAD)
            for i in range(len(sizes_out)):
                outs[i][:, o_at] = acc[
                    starts_out[i] : starts_out[i] + sizes_out[i], :
                ].astype(BF16)

        for g in range(max(heads - 2, 0), heads):
            for c, h in items:
                store(g, g % 2, c, h).wait()

    vmem = pl.BlockSpec(memory_space=pltpu.VMEM)
    hbm = pl.BlockSpec(memory_space=pl.ANY)
    smem = pl.BlockSpec(memory_space=pltpu.SMEM)
    flops = 20 * own * length * group * heads * rows * HEAD
    siblings = pltpu.with_memory_space_constraint(siblings, pltpu.HBM)
    queries = pltpu.with_memory_space_constraint(queries, pltpu.HBM)
    grad_out = pltpu.with_memory_space_constraint(grad_out, pltpu.HBM)
    args = [siblings, me, queries, grad_out, *kv_parts] + ([before] if before is not None else [])
    res = pl.pallas_call(
        kern,
        in_specs=[hbm, smem, hbm, hbm]
        + [vmem] * len(sizes)
        + ([hbm] if before is not None else []),
        out_specs=[hbm] + [vmem] * len(sizes_out),
        scratch_shapes=[
            pltpu.VMEM((total, kvw2), BF16),
            pltpu.VMEM((own, rows, HEAD), BF16),
            pltpu.VMEM((own, rows, HEAD), BF16),
            pltpu.VMEM((total, 2 * HEAD), F32),
            pltpu.VMEM((2, own, length, span), BF16),
            pltpu.VMEM((2, own, length, span), BF16),
            pltpu.VMEM((2, own, length, span), BF16),
            pltpu.SMEM((own, sib), jnp.int32),
            pltpu.SMEM((own, sib), jnp.int32),
            pltpu.SemaphoreType.DMA(()),
            pltpu.SemaphoreType.DMA((2, own, group, 2)),
            pltpu.SemaphoreType.DMA((2, own, group)),
        ],
        out_shape=[jax.ShapeDtypeStruct(queries.shape, BF16)]
        + [jax.ShapeDtypeStruct((size, kvw2), BF16) for size in sizes_out],
        input_output_aliases={4 + len(sizes): 0} if before is not None else {},
        compiler_params=pltpu.CompilerParams(vmem_limit_bytes=VMEM_LIMIT),
        cost_estimate=pl.CostEstimate(
            flops=flops, bytes_accessed=6 * queries.size, transcendentals=0
        ),
        name="attention",
    )(*args)
    return res[0], res[1:]


def add_split(parts, pieces):
    shape = parts[0].shape
    each = shape[0] // pieces
    count = len(parts)

    def kern(*refs):
        for i in range(pieces):
            at = slice(i * each, (i + 1) * each)
            total = refs[0][at].astype(F32)
            for r in refs[1:count]:
                total = total + r[at].astype(F32)
            refs[count + i][...] = total.astype(BF16)

    vmem = pl.BlockSpec(memory_space=pltpu.VMEM)
    return pl.pallas_call(
        kern,
        in_specs=[vmem] * count,
        out_specs=[vmem] * pieces,
        out_shape=[jax.ShapeDtypeStruct((each,) + shape[1:], BF16)] * pieces,
        cost_estimate=pl.CostEstimate(
            flops=0, bytes_accessed=2 * count * parts[0].size, transcendentals=0
        ),
        compiler_params=pltpu.CompilerParams(vmem_limit_bytes=8 << 20),
        name="add_split",
    )(*parts)


def by_target(hidden, devices, dps):
    rows, total = hidden.shape
    width = total // (devices * dps)

    def kern(h_ref, o_ref):
        for t in range(devices):
            for d in range(dps):
                lo = (d * devices + t) * width
                o_ref[t, :, d * width : (d + 1) * width] = h_ref[:, lo : lo + width]

    vmem = pl.BlockSpec(memory_space=pltpu.VMEM)
    return pl.pallas_call(
        kern,
        in_specs=[vmem],
        out_specs=vmem,
        out_shape=jax.ShapeDtypeStruct((devices, rows, dps * width), BF16),
        compiler_params=pltpu.CompilerParams(vmem_limit_bytes=8 << 20),
        name="by_target",
    )(hidden)


def weight_parts(place, columns, grads, heads_of, kv_heads, dps):
    devices, _, wide = columns.shape
    width = wide // dps
    chunks = len(grads)
    parts_of = len(grads[0])
    kvw2 = 2 * kv_heads * HEAD

    def kern(place_ref, c_ref, *refs):
        g_in = [refs[i * parts_of : (i + 1) * parts_of] for i in range(chunks)]
        outs = refs[chunks * parts_of : chunks * parts_of + dps]
        w_s = refs[chunks * parts_of + dps]
        cols = jnp.concatenate([c_ref[place_ref[dps + n]] for n in range(devices)], axis=0)
        col = 0
        for n in range(chunks):
            span = 2 * heads_of[n] * HEAD
            terms = jnp.concatenate([g_in[n][i][...] for i in range(parts_of)], axis=0)
            w_s[:, col : col + span] = dg(cols, terms, 0, 0)
            col += span
        for k in range(dps):
            at = pl.ds(pl.multiple_of(place_ref[k] * width, 8), width)
            for h in range(kv_heads):
                lo = 2 * h * HEAD
                outs[k][:, h * HEAD : (h + 1) * HEAD] = w_s[at, lo : lo + HEAD]
                outs[k][:, (kv_heads + h) * HEAD : (kv_heads + h + 1) * HEAD] = w_s[
                    at, lo + HEAD : lo + 2 * HEAD
                ]

    vmem = pl.BlockSpec(memory_space=pltpu.VMEM)
    return pl.pallas_call(
        kern,
        in_specs=[pl.BlockSpec(memory_space=pltpu.SMEM)] + [vmem] * (1 + chunks * parts_of),
        out_specs=[vmem] * dps,
        out_shape=[jax.ShapeDtypeStruct((width, kvw2), F32)] * dps,
        scratch_shapes=[
            pltpu.VMEM((wide, kvw2), F32),
        ],
        compiler_params=pltpu.CompilerParams(vmem_limit_bytes=32 << 20),
        name="weight_parts",
    )(place, columns, *[g for part in grads for g in part])


def make_per_device(n_seq, n_dp):
    inner = n_seq // OUTER

    def swap(x, axis, count, by):
        return lax.ppermute(x, axis, [(i, i ^ by) for i in range(count)])

    def seq_swap(x, by):
        return swap(x, "seq", n_seq, by)

    def gather_all(x, early):
        rest = [seq_swap(x, k * inner) for k in range(1, OUTER)]
        if not early:
            rest = jnp.concatenate([x] + rest, axis=0)
            return [rest] + [seq_swap(rest, k) for k in range(1, inner)]
        ones = [x] + [seq_swap(x, k) for k in range(1, inner)]
        rest = jnp.concatenate(rest, axis=0)
        rests = [rest] + [seq_swap(rest, k) for k in range(1, inner)]
        return [part for pair in zip(ones, rests, strict=True) for part in pair]

    def per_device(siblings, queries, grad_out, keys_in, input_values, summary):
        own, pos, kvw = keys_in.shape[1:]
        kv_heads = kvw // HEAD
        me = lax.axis_index("seq").astype(jnp.int32)
        me_dp = lax.axis_index("dp").astype(jnp.int32)

        hidden = by_target(summary[0].reshape(own * pos, summary.shape[3]), n_seq, n_dp)
        columns = lax.all_to_all(hidden, "seq", split_axis=0, concat_axis=0, tiled=True)

        kv_parts = []
        first = 0
        for heads in CHUNKS:
            at = slice(first * HEAD, (first + heads) * HEAD)
            kv_parts.append(
                gather_all(
                    jnp.concatenate(
                        [keys_in[0, :, :, at], input_values[0, :, :, at]], axis=-1
                    ).reshape(own * pos, 2 * heads * HEAD),
                    EARLY["rows"],
                )
            )
            first += heads

        query_grad = None
        grads = []
        first = 0
        for n, heads in enumerate(CHUNKS):
            query_grad, terms = attention(
                siblings[0],
                me[None],
                queries[0],
                grad_out[0],
                 kv_parts[n],
                ([own * pos, (OUTER - 1) * own * pos] if EARLY["sum"] else [OUTER * own * pos])
                * inner,
                pos, first, heads, kv_heads, query_grad
            )
            first += heads
            ones, rests = (terms[::2], terms[1::2]) if EARLY["sum"] else ([], terms)
            near = add_split(
                [rests[0]] + [seq_swap(rests[k], k) for k in range(1, inner)],
                rests[0].shape[0] // (own * pos),
            )
            here = [ones[0]] if EARLY["sum"] else [near[0]]
            here += [seq_swap(ones[k], k) for k in range(1, len(ones))]
            away = near if EARLY["sum"] else near[1:]
            here += [seq_swap(away[k - 1], k * inner) for k in range(1, OUTER)]
            mine = add_split(here, 1)[0]
            grads.append(gather_all(mine, EARLY["grads"]))

        dps = jnp.bitwise_xor(jnp.arange(n_dp, dtype=jnp.int32), me_dp)
        order = jnp.array(
            [o * inner + i for i in range(inner) for o in range(OUTER)], dtype=jnp.int32
        )
        place = jnp.concatenate([dps, jnp.bitwise_xor(order, me)])
        parts = weight_parts(place, columns, grads, CHUNKS, kv_heads, n_dp)
        total = parts[0]
        for k in range(1, n_dp):
            total = total + swap(parts[k], "dp", n_dp, k)
        return query_grad[None], total

    return per_device


def solution(mesh):
    rows = P("dp", "seq", None, None)
    return jax.shard_map(
        make_per_device(mesh.shape["seq"], mesh.shape["dp"]),
        mesh=mesh,
        in_specs=(P("dp", "seq", None), rows, rows, rows, rows, rows),
        out_specs=(rows, P(("dp", "seq"), None)),
        check_vma=False,
    )
```
